32 devices in a mesh: shot: 8 (over z, y), xline: 4 (over x, core).
Axes of the slice: x: 2, y: 2, z: 4, core: 2. Of those that a mesh axis runs over, the one named last changes fastest.
Arguments:
- records: bfloat16 [4, 16, 256, 2048], P('xline', 'shot'), may hold values from -1.796875 to 1.796875
- targets: bfloat16 [2048, 32, 256], P('xline', 'shot'), may hold values from -1.796875 to 1.796875
- aperture: int32 [32, 4, 16], P('shot', 'xline'), may hold values from 0 to 255
Outputs:
- multiples: bfloat16 [2048, 32, 256], P('xline', 'shot')
The draws below stay inside these ranges and needn't reach their ends.
Inputs may be any that keep to these rules, and one draw needn't show every extreme that they name: An aperture entry is the receiver of the output shot at which the contributing source lies.
All inputs are finite; a program needn't handle non-finite values.
Results may differ from the reference program's by a relative error of at most 0.0071.
Values may be sent and summed in bfloat16 or wider, within the bound.
A program may use at most 128 MiB of HBM per device.

```python
import math
import jax
import jax.numpy as jnp
from jax import lax

R = 256
NT = 2048
NF = 256
NS = 32
NC = 16
NL = 4


def with_ends(result, key, low, high):
    dims = result.shape
    index_at = [jax.random.randint(jax.random.fold_in(key, axis), (), 0, dims[axis]) for axis in range(len(dims))]
    result = result.at[tuple(index_at)].set(low)
    longest = dims.index(max(dims))
    index_at[longest] = (index_at[longest] + 1) % dims[longest]
    return result.at[tuple(index_at)].set(high)


def level_of(rng, extent, shards, least, high):
    level = 1.0
    for dim, parts in shards:
        steps = jax.random.uniform(jax.random.fold_in(jax.random.fold_in(rng, 6), dim), (parts,), jnp.float32, least / len(shards), high / len(shards))
        level = level * jnp.repeat(jnp.exp(steps), extent[dim] // parts).reshape((-1,) + (1,) * (len(extent) - 1 - dim))
    return level


def gaussian(own_key, dims, deviation, bound, cuts=(), held_as=jnp.bfloat16):
    result = deviation * jax.random.normal(own_key, dims, jnp.float32)
    if cuts:
        result = result * level_of(own_key, dims, cuts, -0.22, 0.18)
    return jnp.clip(result, -bound, bound).astype(held_as)


def setup_inputs(seed: int = 0) -> dict:
    splits = jax.random.split(jax.random.key(seed), 4)
    records = gaussian(splits[0], (NL, NC, R, NT), 0.3, 1.796875, ((0, 4), (1, 8)))
    targets = gaussian(splits[1], (NT, NS, R), 0.3, 1.796875, ((0, 4), (1, 8)))
    aperture = with_ends(jax.random.randint(splits[2], (NS, NL, NC), 0, R), jax.random.fold_in(splits[2], 1), 0, R - 1).astype(jnp.int32)
    return dict(records=records, targets=targets, aperture=aperture)


def forward_table():
    times_col = jnp.arange(NT, dtype=jnp.int32)[:, None]
    freq_row = jnp.arange(1, NF + 1, dtype=jnp.int32)[None, :]
    angles = (times_col * freq_row % NT).astype(jnp.float32) * (2.0 * math.pi / NT)
    normalizing_scale = 1.0 / math.sqrt(NT)
    return jnp.concatenate([jnp.cos(angles) * normalizing_scale, -jnp.sin(angles) * normalizing_scale], axis=1).astype(jnp.bfloat16)

def inverse_table():
    times_col = jnp.arange(NT, dtype=jnp.int32)[:, None]
    freq_row = jnp.arange(1, NF + 1, dtype=jnp.int32)[None, :]
    angles = (times_col * freq_row % NT).astype(jnp.float32) * (2.0 * math.pi / NT)
    normalizing_scale = 2.0 / math.sqrt(NT)
    stacked = jnp.stack([jnp.cos(angles) * normalizing_scale, -jnp.sin(angles) * normalizing_scale], axis=2)
    return stacked.reshape(NT, 2 * NF)

def complex_mixing(real_part, imag_part):
    upper = jnp.stack([real_part, -imag_part], axis=1)
    lower = jnp.stack([imag_part, real_part], axis=1)
    return jnp.stack([upper, lower], axis=0)

def reference(records, targets, aperture):
    forward_fourier = forward_table().astype(jnp.float32)
    desired_spectra = jnp.einsum('tsr,tp->srp', targets.astype(jnp.float32), forward_fourier).astype(jnp.bfloat16)
    running = jnp.zeros((NF, 2, NS, R), jnp.float32)
    receivers = jnp.arange(R, dtype=jnp.int32)
    for source_line in range(NL):
        trace_spectra = jnp.einsum('crt,tp->cpr', records[source_line].astype(jnp.float32), forward_fourier)
        trace_spectra = trace_spectra.astype(jnp.bfloat16).reshape(NC, 2, NF, R)
        onehot = (aperture[:, source_line, :, None] == receivers).astype(jnp.float32)
        picked = jnp.einsum('scr,srp->scp', onehot, desired_spectra.astype(jnp.float32))
        mixing = complex_mixing(picked[:, :, :NF], picked[:, :, NF:])
        running = running + jnp.einsum('qspcf,cpfr->fqsr', mixing, trace_spectra.astype(jnp.float32))
    flat_traces = running.reshape(2 * NF, NS * R)
    predicted = jnp.dot(inverse_table(), flat_traces, precision=lax.Precision.HIGHEST, preferred_element_type=jnp.float32)
    return predicted.reshape(NT, NS, R).astype(jnp.bfloat16)
```

```python
import math

import jax
import jax.numpy as jnp
from jax import lax
from jax.sharding import PartitionSpec as P

NT = 2048
NF = 256
LOW = 32


def fourier_table(bins):
    blocks = NF // bins
    freq = jnp.arange(1, NF + 1, dtype=jnp.int32).reshape(blocks, 1, bins)
    freq = jnp.broadcast_to(freq, (blocks, 2, bins)).reshape(1, 2 * NF)
    is_imag = jnp.arange(2, dtype=jnp.int32).reshape(1, 2, 1)
    is_imag = jnp.broadcast_to(is_imag, (blocks, 2, bins)).reshape(1, 2 * NF) == 1

    def trig(times):
        angles = (times[:, None] * freq % NT).astype(jnp.float32) * (2.0 * math.pi / NT)
        return jnp.cos(angles), jnp.sin(angles)

    cos_hi, sin_hi = trig(jnp.arange(NT // LOW, dtype=jnp.int32) * LOW)
    cos_lo, sin_lo = trig(jnp.arange(LOW, dtype=jnp.int32))
    scale = 1.0 / math.sqrt(NT)
    first = jnp.where(is_imag, -sin_hi, cos_hi) * scale
    second = jnp.where(is_imag, -cos_hi, -sin_hi) * scale
    first, second, cos_lo, sin_lo = lax.optimization_barrier((first, second, cos_lo, sin_lo))
    table = first[:, None] * cos_lo[None] + second[:, None] * sin_lo[None]
    return table.reshape(NT, 2 * NF).astype(jnp.bfloat16)


def on_device(records, targets, aperture):
    f32, bf16 = jnp.float32, jnp.bfloat16
    lines = lax.axis_size("xline")
    columns = lax.axis_size("shot")
    devices = lines * columns
    bins = NF // devices
    time_rows, shots, receivers = targets.shape
    held = records.shape[1]
    gathers = aperture.shape[2]
    table = fourier_table(bins)

    apertures = lax.all_to_all(
        jnp.broadcast_to(aperture.reshape(1, shots, gathers), (lines, shots, gathers)),
        "xline", 0, 0, tiled=True,
    )
    receiver_ids = jnp.arange(receivers, dtype=jnp.int32)
    chosen = apertures.transpose(1, 0, 2).reshape(shots, lines * gathers)
    onehot = (chosen[:, :, None] == receiver_ids).astype(bf16)
    traces = jnp.einsum("skr,tsr->skt", onehot, targets, preferred_element_type=f32).astype(bf16)
    traces = traces.reshape(shots, lines, gathers, time_rows).transpose(1, 0, 2, 3)
    traces = lax.all_to_all(
        traces.reshape(lines, shots * gathers, time_rows), "xline", 0, 0, tiled=True
    )
    traces = traces.transpose(1, 0, 2).reshape(shots * gathers, NT)
    picked = jnp.einsum("tp,kt->pk", table, traces, preferred_element_type=f32).astype(bf16)

    spectra = jnp.einsum(
        "tp,kt->pk", table, records.reshape(held * receivers, NT), preferred_element_type=f32
    ).astype(bf16)

    width = held * receivers
    both = jnp.concatenate([spectra, picked], axis=1).reshape(devices, 2 * bins, -1)
    both = lax.all_to_all(both, ("xline", "shot"), 0, 0, tiled=True)
    spectra = both[:, :, :width].reshape(devices, 2 * bins, held, receivers)
    picked = both[:, :, width:].reshape(lines, columns, 2, bins, shots, columns, held)

    real, imag = picked[:, :, 0], picked[:, :, 1]
    mixing = jnp.stack(
        [jnp.stack([real, -imag], 0), jnp.stack([imag, real], 0)], 0
    )
    eye = jnp.eye(bins, dtype=bf16)
    mixing = jnp.einsum("xqldfsch,fg->dxfslcqgh", mixing, eye).astype(bf16)
    mixing = mixing.reshape(columns * 2 * bins * shots, devices, 2 * bins, held)
    running = jnp.einsum(
        "mvph,vphr->mr", mixing, spectra, preferred_element_type=f32
    ).astype(bf16)
    running = running.reshape(columns, 2 * bins * shots, receivers)
    running = lax.all_to_all(running, "shot", 0, 0, tiled=True)
    running = lax.all_gather(running, "xline", axis=0, tiled=True)
    running = running.reshape(2 * NF, shots, receivers)

    rows = lax.dynamic_slice_in_dim(table, lax.axis_index("xline") * time_rows, time_rows, 0)
    out = jnp.einsum("tp,psr->tsr", rows * 2, running, preferred_element_type=f32)
    return out.astype(bf16)


def solution(mesh):
    in_specs = (P("xline", "shot", None, None), P("xline", "shot", None), P("shot", "xline", None))
    out_specs = P("xline", "shot", None)
    return jax.shard_map(
        on_device, mesh=mesh, in_specs=in_specs, out_specs=out_specs, check_vma=False
    )
```

```python
import functools
import math

import jax
import jax.numpy as jnp
from jax import lax
from jax.experimental import pallas as pl
from jax.experimental.pallas import tpu as pltpu
from jax.sharding import PartitionSpec as P

NT = 2048
NF = 256
LOW = 32


def fourier_table(bins):
    blocks = NF // bins
    freq = jnp.arange(1, NF + 1, dtype=jnp.int32).reshape(blocks, 1, bins)
    freq = jnp.broadcast_to(freq, (blocks, 2, bins)).reshape(1, 2 * NF)
    is_imag = jnp.arange(2, dtype=jnp.int32).reshape(1, 2, 1)
    is_imag = jnp.broadcast_to(is_imag, (blocks, 2, bins)).reshape(1, 2 * NF) == 1

    def trig(times):
        angles = (times[:, None] * freq % NT).astype(jnp.float32) * (2.0 * math.pi / NT)
        return jnp.cos(angles), jnp.sin(angles)

    cos_hi, sin_hi = trig(jnp.arange(NT // LOW, dtype=jnp.int32) * LOW)
    cos_lo, sin_lo = trig(jnp.arange(LOW, dtype=jnp.int32))
    scale = 1.0 / math.sqrt(NT)
    first = jnp.where(is_imag, -sin_hi, cos_hi) * scale
    second = jnp.where(is_imag, -cos_hi, -sin_hi) * scale
    first, second, cos_lo, sin_lo = lax.optimization_barrier((first, second, cos_lo, sin_lo))
    table = first[:, None] * cos_lo[None] + second[:, None] * sin_lo[None]
    return table.reshape(NT, 2 * NF).astype(jnp.bfloat16)


def mix_kernel(lines, columns, held, bins, shots, spectra_ref, picked_ref, out_ref):
    gathers = columns * held
    receivers = out_ref.shape[1]
    rows = columns * bins
    depth = columns * 2 * bins
    taken = 2 * shots * gathers
    wide = held * depth

    k = lax.broadcasted_iota(jnp.int32, (taken, wide), 0)
    j = lax.broadcasted_iota(jnp.int32, (taken, wide), 1)
    k_imag, k_shot, k_gather = k // (shots * gathers), k // gathers % shots, k % gathers
    j_held, j_column, j_imag = j // depth, j % depth // (2 * bins), j // bins % 2
    same = k_gather == j_column * held + j_held
    crossed = k_imag != j_imag
    expand = []
    for shot in range(shots):
        for part in range(2):
            hit = same & (k_shot == shot) & (crossed if part else ~crossed)
            value = jnp.where(hit, 1.0, 0.0)
            if part == 0:
                value = jnp.where(j_imag == 1, -value, value)
            expand.append(value.astype(jnp.bfloat16))
    bin_of_row = lax.broadcasted_iota(jnp.int32, (rows, wide), 0) % bins
    bin_of_column = lax.broadcasted_iota(jnp.int32, (rows, wide), 1) % bins
    same_bin = bin_of_row == bin_of_column

    total = jnp.zeros(out_ref.shape, jnp.float32)
    for line in range(lines):
        block = picked_ref[line * rows : (line + 1) * rows, :]
        mixing = [
            jnp.where(
                same_bin, jnp.dot(block, matrix, preferred_element_type=jnp.float32), 0.0
            ).astype(jnp.bfloat16)
            for matrix in expand
        ]
        held_rows = slice(line * depth, (line + 1) * depth)
        spectra = jnp.concatenate(
            [spectra_ref[held_rows, h * receivers : (h + 1) * receivers] for h in range(held)], axis=0
        )
        total += jnp.dot(
            jnp.concatenate(mixing, axis=0), spectra, preferred_element_type=jnp.float32
        )
    out_ref[...] = total.astype(out_ref.dtype)


def on_device(records, targets, aperture):
    f32, bf16 = jnp.float32, jnp.bfloat16
    lines = lax.axis_size("xline")
    columns = lax.axis_size("shot")
    devices = lines * columns
    bins = NF // devices
    time_rows, shots, receivers = targets.shape
    held = records.shape[1]
    gathers = aperture.shape[2]
    table = fourier_table(bins)

    apertures = lax.all_to_all(
        jnp.broadcast_to(aperture.reshape(1, shots, gathers), (lines, shots, gathers)),
        "xline", 0, 0, tiled=True,
    )
    receiver_ids = jnp.arange(receivers, dtype=jnp.int32)
    chosen = apertures.transpose(1, 0, 2).reshape(shots, lines * gathers)
    onehot = (chosen[:, :, None] == receiver_ids).astype(bf16)
    traces = jnp.einsum("skr,tsr->skt", onehot, targets, preferred_element_type=f32).astype(bf16)
    traces = traces.reshape(shots, lines, gathers, time_rows).transpose(1, 0, 2, 3)
    traces = lax.all_to_all(
        traces.reshape(lines, shots * gathers, time_rows), "xline", 0, 0, tiled=True
    )
    traces = traces.transpose(1, 0, 2).reshape(shots * gathers, NT)
    picked = jnp.einsum("tp,kt->pk", table, traces, preferred_element_type=f32).astype(bf16)

    spectra = jnp.einsum(
        "tp,kt->pk", table, records.reshape(held * receivers, NT), preferred_element_type=f32
    ).astype(bf16)

    spectra = spectra.reshape(devices, 2 * bins, held * receivers)
    spectra = lax.all_to_all(spectra, ("xline", "shot"), 0, 0, tiled=True)
    picked = picked.reshape(devices, 2, bins, shots * gathers)
    picked = jnp.concatenate([picked[:, 0], picked[:, 1]], axis=-1)
    picked = lax.all_to_all(picked, ("xline", "shot"), 0, 0, tiled=True)

    running = pl.pallas_call(
        functools.partial(mix_kernel, lines, columns, held, bins, shots),
        out_shape=jax.ShapeDtypeStruct((shots * 2 * columns * bins, receivers), bf16),
        in_specs=[pl.BlockSpec(memory_space=pltpu.VMEM)] * 2,
        out_specs=pl.BlockSpec(memory_space=pltpu.VMEM),
    )(spectra.reshape(2 * NF, held * receivers), picked.reshape(NF, -1))
    running = running.reshape(shots, 2, columns, bins, receivers).transpose(2, 0, 1, 3, 4)
    running = running.reshape(columns, shots, 2 * bins, receivers)
    running = lax.all_to_all(running, "shot", 0, 0, tiled=True)
    running = lax.all_gather(running, "xline", axis=0, tiled=True)
    running = running.transpose(0, 2, 1, 3).reshape(2 * NF, shots, receivers)

    rows = lax.dynamic_slice_in_dim(table, lax.axis_index("xline") * time_rows, time_rows, 0)
    out = jnp.einsum("tp,psr->tsr", rows * 2, running, preferred_element_type=f32)
    return out.astype(bf16)


def solution(mesh):
    in_specs = (P("xline", "shot", None, None), P("xline", "shot", None), P("shot", "xline", None))
    out_specs = P("xline", "shot", None)
    return jax.shard_map(
        on_device, mesh=mesh, in_specs=in_specs, out_specs=out_specs, check_vma=False
    )
```

```python
import functools
import math

import jax
import jax.numpy as jnp
from jax import lax
from jax.experimental import pallas as pl
from jax.experimental.pallas import tpu as pltpu
from jax.sharding import PartitionSpec as P

NT = 2048
NF = 256
LOW = 32


def fourier_table(bins):
    blocks = NF // bins
    freq = jnp.arange(1, NF + 1, dtype=jnp.int32).reshape(blocks, 1, bins)
    freq = jnp.broadcast_to(freq, (blocks, 2, bins)).reshape(1, 2 * NF)
    is_imag = jnp.arange(2, dtype=jnp.int32).reshape(1, 2, 1)
    is_imag = jnp.broadcast_to(is_imag, (blocks, 2, bins)).reshape(1, 2 * NF) == 1

    def trig(times):
        angles = (times[:, None] * freq % NT).astype(jnp.float32) * (2.0 * math.pi / NT)
        return jnp.cos(angles), jnp.sin(angles)

    cos_hi, sin_hi = trig(jnp.arange(NT // LOW, dtype=jnp.int32) * LOW)
    cos_lo, sin_lo = trig(jnp.arange(LOW, dtype=jnp.int32))
    scale = 1.0 / math.sqrt(NT)
    first = jnp.where(is_imag, -sin_hi, cos_hi) * scale
    second = jnp.where(is_imag, -cos_hi, -sin_hi) * scale
    first, second, cos_lo, sin_lo = lax.optimization_barrier((first, second, cos_lo, sin_lo))
    table = first[:, None] * cos_lo[None] + second[:, None] * sin_lo[None]
    return table.reshape(NT, 2 * NF).astype(jnp.bfloat16)


def mix_kernel(lines, columns, held, bins, shots, spectra_ref, picked_ref, out_ref):
    gathers = columns * held
    receivers = out_ref.shape[1]
    rows = columns * bins
    depth = columns * 2 * bins
    taken = 2 * shots * gathers
    wide = held * depth

    k = lax.broadcasted_iota(jnp.int32, (taken, wide), 0)
    j = lax.broadcasted_iota(jnp.int32, (taken, wide), 1)
    k_imag, k_shot, k_gather = k // (shots * gathers), k // gathers % shots, k % gathers
    j_held, j_column, j_imag = j // depth, j % depth // (2 * bins), j // bins % 2
    same = k_gather == j_column * held + j_held
    crossed = k_imag != j_imag
    expand = []
    for shot in range(shots):
        for part in range(2):
            hit = same & (k_shot == shot) & (crossed if part else ~crossed)
            value = jnp.where(hit, 1.0, 0.0)
            if part == 0:
                value = jnp.where(j_imag == 1, -value, value)
            expand.append(value.astype(jnp.bfloat16))
    bin_of_row = lax.broadcasted_iota(jnp.int32, (rows, wide), 0) % bins
    bin_of_column = lax.broadcasted_iota(jnp.int32, (rows, wide), 1) % bins
    same_bin = bin_of_row == bin_of_column

    total = jnp.zeros(out_ref.shape, jnp.float32)
    for line in range(lines):
        block = picked_ref[line * rows : (line + 1) * rows, :]
        mixing = [
            jnp.where(
                same_bin, jnp.dot(block, matrix, preferred_element_type=jnp.float32), 0.0
            ).astype(jnp.bfloat16)
            for matrix in expand
        ]
        held_rows = slice(line * depth, (line + 1) * depth)
        spectra = jnp.concatenate(
            [spectra_ref[held_rows, h * receivers : (h + 1) * receivers] for h in range(held)], axis=0
        )
        total += jnp.dot(
            jnp.concatenate(mixing, axis=0), spectra, preferred_element_type=jnp.float32
        )
    out_ref[...] = total.astype(out_ref.dtype)


def spread_kernel(lines, columns, spectra_ref, picked_ref, spectra_out, picked_out, send, recv, own):
    devices = lines * columns
    me = lax.axis_index("xline") * columns + lax.axis_index("shot")
    mesh_id = pl.DeviceIdType.MESH
    barrier = pltpu.get_barrier_semaphore()

    def greet(step, _):
        peer = lax.rem(me + step, devices)
        pl.semaphore_signal(
            barrier, inc=1,
            device_id={"xline": peer // columns, "shot": lax.rem(peer, columns)},
            device_id_type=mesh_id,
        )
        return 0

    lax.fori_loop(1, devices, greet, 0)
    pl.semaphore_wait(barrier, devices - 1)

    def copies(step):
        peer = lax.rem(me + step, devices)
        return [
            pltpu.make_async_remote_copy(
                src_ref=source.at[peer],
                dst_ref=target.at[me],
                send_sem=send.at[which, step],
                recv_sem=recv.at[which, step],
                device_id={"xline": peer // columns, "shot": lax.rem(peer, columns)},
                device_id_type=mesh_id,
            )
            for which, (source, target) in enumerate(
                ((spectra_ref, spectra_out), (picked_ref, picked_out))
            )
        ]

    def begin(step, _):
        for copy in copies(step):
            copy.start()
        return 0

    def finish(step, _):
        for copy in copies(step):
            copy.wait_send()
        origin = lax.rem(me + devices - step, devices)
        for which, target in enumerate((spectra_out, picked_out)):
            pltpu.make_async_remote_copy(
                src_ref=target.at[origin],
                dst_ref=target.at[origin],
                send_sem=send.at[which, step],
                recv_sem=recv.at[which, step],
                device_id={"xline": origin // columns, "shot": lax.rem(origin, columns)},
                device_id_type=mesh_id,
            ).wait_recv()
        return 0

    lax.fori_loop(1, devices, begin, 0)
    mine = [
        pltpu.make_async_copy(spectra_ref.at[me], spectra_out.at[me], own.at[0]),
        pltpu.make_async_copy(picked_ref.at[me], picked_out.at[me], own.at[1]),
    ]
    for copy in mine:
        copy.start()
    for copy in mine:
        copy.wait()
    lax.fori_loop(1, devices, finish, 0)


def collect_kernel(lines, columns, running_ref, out_ref, send, recv, own):
    line = lax.axis_index("xline")
    me = lax.axis_index("shot")
    core_line = line + 1 - 2 * lax.rem(line, 2)
    far_line = lax.rem(line + lines // 2, lines)
    diagonal_line = lax.rem(core_line + lines // 2, lines)
    mesh_id = pl.DeviceIdType.MESH
    barrier = pltpu.get_barrier_semaphore()

    def greet(step, _):
        pl.semaphore_signal(
            barrier, inc=1, device_id={"shot": lax.rem(me + step, columns)}, device_id_type=mesh_id
        )
        return 0

    lax.fori_loop(1, columns, greet, 0)
    for peer in (core_line, far_line):
        pl.semaphore_signal(barrier, inc=1, device_id={"xline": peer}, device_id_type=mesh_id)
    pl.semaphore_wait(barrier, columns + 1)

    def across(step):
        peer = lax.rem(me + step, columns)
        return pltpu.make_async_remote_copy(
            src_ref=running_ref.at[peer],
            dst_ref=out_ref.at[line * columns + me],
            send_sem=send.at[0, step],
            recv_sem=recv.at[0, step],
            device_id={"shot": peer},
            device_id_type=mesh_id,
        )

    def onward(stage, source_line, peer_line, step):
        slot = source_line * columns + lax.rem(me + columns - step, columns)
        return pltpu.make_async_remote_copy(
            src_ref=out_ref.at[slot],
            dst_ref=out_ref.at[slot],
            send_sem=send.at[stage, step],
            recv_sem=recv.at[stage, step],
            device_id={"xline": peer_line},
            device_id_type=mesh_id,
        )

    def begin(step, _):
        across(step).start()
        return 0

    lax.fori_loop(1, columns, begin, 0)
    mine = pltpu.make_async_copy(running_ref.at[me], out_ref.at[line * columns + me], own.at[0])
    mine.start()
    mine.wait()
    onward(2, line, far_line, 0).start()
    onward(1, line, core_line, 0).start()

    def relay(step, _):
        slot = line * columns + lax.rem(me + columns - step, columns)
        pltpu.make_async_remote_copy(
            src_ref=out_ref.at[slot],
            dst_ref=out_ref.at[slot],
            send_sem=send.at[0, step],
            recv_sem=recv.at[0, step],
            device_id={"shot": lax.rem(me + columns - step, columns)},
            device_id_type=mesh_id,
        ).wait_recv()
        onward(2, line, far_line, step).start()
        onward(1, line, core_line, step).start()
        return 0

    lax.fori_loop(1, columns, relay, 0)

    def turn(step, _):
        onward(2, far_line, far_line, step).wait_recv()
        onward(3, far_line, core_line, step).start()
        return 0

    lax.fori_loop(0, columns, turn, 0)

    def finish(step, _):
        onward(1, core_line, core_line, step).wait_recv()
        onward(3, diagonal_line, core_line, step).wait_recv()
        onward(1, line, core_line, step).wait_send()
        onward(2, line, far_line, step).wait_send()
        onward(3, far_line, core_line, step).wait_send()
        return 0

    lax.fori_loop(0, columns, finish, 0)

    def sent(step, _):
        across(step).wait_send()
        return 0

    lax.fori_loop(1, columns, sent, 0)


def on_device(records, targets, aperture):
    f32, bf16 = jnp.float32, jnp.bfloat16
    lines = lax.axis_size("xline")
    columns = lax.axis_size("shot")
    devices = lines * columns
    bins = NF // devices
    time_rows, shots, receivers = targets.shape
    held = records.shape[1]
    gathers = aperture.shape[2]
    table = fourier_table(bins)

    apertures = lax.all_to_all(
        jnp.broadcast_to(aperture.reshape(1, shots, gathers), (lines, shots, gathers)),
        "xline", 0, 0, tiled=True,
    )
    receiver_ids = jnp.arange(receivers, dtype=jnp.int32)
    chosen = apertures.transpose(1, 0, 2).reshape(shots, lines * gathers)
    onehot = (chosen[:, :, None] == receiver_ids).astype(bf16)
    traces = jnp.einsum("skr,tsr->skt", onehot, targets, preferred_element_type=f32).astype(bf16)
    traces = traces.reshape(shots, lines, gathers, time_rows).transpose(1, 0, 2, 3)
    traces = lax.all_to_all(
        traces.reshape(lines, shots * gathers, time_rows), "xline", 0, 0, tiled=True
    )
    traces = traces.transpose(1, 0, 2).reshape(shots * gathers, NT)
    picked = jnp.einsum("tp,kt->pk", table, traces, preferred_element_type=f32).astype(bf16)

    spectra = jnp.einsum(
        "tp,kt->pk", table, records.reshape(held * receivers, NT), preferred_element_type=f32
    ).astype(bf16)

    spectra = spectra.reshape(devices, 2 * bins, held * receivers)
    picked = picked.reshape(devices, 2, bins, shots * gathers)
    picked = jnp.concatenate([picked[:, 0], picked[:, 1]], axis=-1)
    in_vmem = pl.BlockSpec(memory_space=pltpu.VMEM)
    dma = pltpu.SemaphoreType.DMA
    spectra, picked = pl.pallas_call(
        functools.partial(spread_kernel, lines, columns),
        out_shape=[
            jax.ShapeDtypeStruct(spectra.shape, bf16),
            jax.ShapeDtypeStruct(picked.shape, bf16),
        ],
        in_specs=[in_vmem] * 2,
        out_specs=[in_vmem] * 2,
        scratch_shapes=[dma((2, devices)), dma((2, devices)), dma((2,))],
        compiler_params=pltpu.CompilerParams(collective_id=0, has_side_effects=True),
    )(spectra, picked)

    running = pl.pallas_call(
        functools.partial(mix_kernel, lines, columns, held, bins, shots),
        out_shape=jax.ShapeDtypeStruct((shots * 2 * columns * bins, receivers), bf16),
        in_specs=[pl.BlockSpec(memory_space=pltpu.VMEM)] * 2,
        out_specs=pl.BlockSpec(memory_space=pltpu.VMEM),
    )(spectra.reshape(2 * NF, held * receivers), picked.reshape(NF, -1))
    running = running.reshape(shots, 2, columns, bins, receivers).transpose(2, 0, 1, 3, 4)
    running = running.reshape(columns, shots, 2 * bins, receivers)
    running = pl.pallas_call(
        functools.partial(collect_kernel, lines, columns),
        out_shape=jax.ShapeDtypeStruct((devices, *running.shape[1:]), bf16),
        in_specs=[in_vmem],
        out_specs=in_vmem,
        scratch_shapes=[dma((4, columns)), dma((4, columns)), dma((1,))],
        compiler_params=pltpu.CompilerParams(collective_id=1, has_side_effects=True),
    )(running)
    running = running.transpose(0, 2, 1, 3).reshape(2 * NF, shots, receivers)

    rows = lax.dynamic_slice_in_dim(table, lax.axis_index("xline") * time_rows, time_rows, 0)
    out = jnp.einsum("tp,psr->tsr", rows * 2, running, preferred_element_type=f32)
    return out.astype(bf16)


def solution(mesh):
    in_specs = (P("xline", "shot", None, None), P("xline", "shot", None), P("shot", "xline", None))
    out_specs = P("xline", "shot", None)
    return jax.shard_map(
        on_device, mesh=mesh, in_specs=in_specs, out_specs=out_specs, check_vma=False
    )
```

```python
import functools
import math

import jax
import jax.numpy as jnp
from jax import lax
from jax.experimental import pallas as pl
from jax.experimental.pallas import tpu as pltpu
from jax.sharding import PartitionSpec as P

NT = 2048
NF = 256
LOW = 32


def fourier_table(bins, start, count):
    blocks = NF // bins
    freq = jnp.arange(1, NF + 1, dtype=jnp.int32).reshape(blocks, 1, bins)
    freq = jnp.broadcast_to(freq, (blocks, 2, bins)).reshape(1, 2 * NF)
    is_imag = jnp.arange(2, dtype=jnp.int32).reshape(1, 2, 1)
    is_imag = jnp.broadcast_to(is_imag, (blocks, 2, bins)).reshape(1, 2 * NF) == 1

    def trig(times):
        angles = (times[:, None] * freq % NT).astype(jnp.float32) * (2.0 * math.pi / NT)
        return jnp.cos(angles), jnp.sin(angles)

    cos_hi, sin_hi = trig(start + jnp.arange(count // LOW, dtype=jnp.int32) * LOW)
    cos_lo, sin_lo = trig(jnp.arange(LOW, dtype=jnp.int32))
    scale = 1.0 / math.sqrt(NT)
    first = jnp.where(is_imag, -sin_hi, cos_hi) * scale
    second = jnp.where(is_imag, -cos_hi, -sin_hi) * scale
    first, second, cos_lo, sin_lo = lax.optimization_barrier((first, second, cos_lo, sin_lo))
    table = first[:, None] * cos_lo[None] + second[:, None] * sin_lo[None]
    return table.reshape(count, 2 * NF).astype(jnp.bfloat16)


def mix_kernel(lines, columns, held, bins, shots, spectra_ref, picked_ref, out_ref):
    gathers = columns * held
    receivers = out_ref.shape[1]
    rows = columns * bins
    depth = columns * 2 * bins
    taken = 2 * shots * gathers
    wide = held * depth

    k = lax.broadcasted_iota(jnp.int32, (taken, wide), 0)
    j = lax.broadcasted_iota(jnp.int32, (taken, wide), 1)
    k_imag, k_shot, k_gather = k // (shots * gathers), k // gathers % shots, k % gathers
    j_held, j_column, j_imag = j // depth, j % depth // (2 * bins), j // bins % 2
    same = k_gather == j_column * held + j_held
    crossed = k_imag != j_imag
    expand = []
    for shot in range(shots):
        for part in range(2):
            hit = same & (k_shot == shot) & (crossed if part else ~crossed)
            value = jnp.where(hit, 1.0, 0.0)
            if part == 0:
                value = jnp.where(j_imag == 1, -value, value)
            expand.append(value.astype(jnp.bfloat16))
    bin_of_row = lax.broadcasted_iota(jnp.int32, (rows, wide), 0) % bins
    bin_of_column = lax.broadcasted_iota(jnp.int32, (rows, wide), 1) % bins
    same_bin = bin_of_row == bin_of_column

    total = jnp.zeros(out_ref.shape, jnp.float32)
    for line in range(lines):
        block = picked_ref[line * rows : (line + 1) * rows, :]
        mixing = [
            jnp.where(
                same_bin, jnp.dot(block, matrix, preferred_element_type=jnp.float32), 0.0
            ).astype(jnp.bfloat16)
            for matrix in expand
        ]
        held_rows = slice(line * depth, (line + 1) * depth)
        spectra = jnp.concatenate(
            [spectra_ref[held_rows, h * receivers : (h + 1) * receivers] for h in range(held)], axis=0
        )
        total += jnp.dot(
            jnp.concatenate(mixing, axis=0), spectra, preferred_element_type=jnp.float32
        )
    out_ref[...] = total.astype(out_ref.dtype)


def spread_kernel(
    lines, columns, gathers, spectra_ref, targets_ref, aperture_ref, table_ref,
    spectra_out, picked_out,
    apertures, traces_here, traces, picked, send, recv, own, line_send, line_recv,
):
    devices = lines * columns
    line = lax.axis_index("xline")
    shots, time_rows, receivers = targets_ref.shape
    chosen = shots * gathers
    me = lax.axis_index("xline") * columns + lax.axis_index("shot")
    mesh_id = pl.DeviceIdType.MESH
    barrier = pltpu.get_barrier_semaphore()

    def greet(step, _):
        peer = lax.rem(me + step, devices)
        pl.semaphore_signal(
            barrier, inc=1,
            device_id={"xline": peer // columns, "shot": lax.rem(peer, columns)},
            device_id_type=mesh_id,
        )
        return 0

    lax.fori_loop(1, devices, greet, 0)
    pl.semaphore_wait(barrier, devices - 1)

    def copy_of(which, source, target, step):
        peer = lax.rem(me + step, devices)
        return pltpu.make_async_remote_copy(
            src_ref=source.at[peer],
            dst_ref=target.at[me],
            send_sem=send.at[which, step],
            recv_sem=recv.at[which, step],
            device_id={"xline": peer // columns, "shot": lax.rem(peer, columns)},
            device_id_type=mesh_id,
        )

    def arrival_of(which, target, step):
        origin = lax.rem(me + devices - step, devices)
        return pltpu.make_async_remote_copy(
            src_ref=target.at[origin],
            dst_ref=target.at[origin],
            send_sem=send.at[which, step],
            recv_sem=recv.at[which, step],
            device_id={"xline": origin // columns, "shot": lax.rem(origin, columns)},
            device_id_type=mesh_id,
        )

    def along_line(which, source, target, step):
        peer = lax.rem(line + step, lines)
        return pltpu.make_async_remote_copy(
            src_ref=source.at[peer] if which else source,
            dst_ref=target.at[line],
            send_sem=line_send.at[which, step],
            recv_sem=line_recv.at[which, step],
            device_id={"xline": peer},
            device_id_type=mesh_id,
        )

    def from_line(which, target, step):
        origin = lax.rem(line + lines - step, lines)
        return pltpu.make_async_remote_copy(
            src_ref=target.at[origin],
            dst_ref=target.at[origin],
            send_sem=line_send.at[which, step],
            recv_sem=line_recv.at[which, step],
            device_id={"xline": origin},
            device_id_type=mesh_id,
        )

    def begin(step, _):
        copy_of(0, spectra_ref, spectra_out, step).start()
        return 0

    for step in range(1, lines):
        along_line(0, aperture_ref, apertures, step).start()
    mine = [
        pltpu.make_async_copy(aperture_ref, apertures.at[line], own.at[0]),
        pltpu.make_async_copy(spectra_ref.at[me], spectra_out.at[me], own.at[1]),
    ]
    for copy in mine:
        copy.start()
    for copy in mine:
        copy.wait()
    for step in range(1, lines):
        from_line(0, apertures, step).wait_recv()

    wanted = jnp.concatenate([apertures[l] for l in range(lines)], axis=1)
    lane = lax.broadcasted_iota(jnp.int32, (receivers, lines * chosen), 1)
    receiver = lax.broadcasted_iota(jnp.int32, (receivers, lines * chosen), 0)
    total = jnp.zeros((time_rows, lines * chosen), jnp.float32)
    for shot in range(shots):
        hit = (lane // gathers % shots == shot) & (receiver == wanted)
        onehot = jnp.where(hit, 1.0, 0.0).astype(jnp.bfloat16)
        total += jnp.dot(targets_ref[shot], onehot, preferred_element_type=jnp.float32)
    total = total.astype(jnp.bfloat16)
    for l in range(lines):
        traces_here[l] = total[:, l * chosen : (l + 1) * chosen]

    lax.fori_loop(1, columns, begin, 0)
    for step in range(1, lines):
        along_line(1, traces_here, traces, step).start()
    lax.fori_loop(columns, devices, begin, 0)
    keep = pltpu.make_async_copy(traces_here.at[line], traces.at[line], own.at[2])
    keep.start()
    keep.wait()
    for step in range(1, lines):
        from_line(1, traces, step).wait_recv()

    value = jnp.zeros((table_ref.shape[0], chosen), jnp.float32)
    for l in range(lines):
        value += jnp.dot(
            table_ref[:, l * time_rows : (l + 1) * time_rows], traces[l],
            preferred_element_type=jnp.float32,
        )
    picked[...] = value.astype(jnp.bfloat16).reshape(picked.shape)
    arrival_of(0, spectra_out, 1).wait_recv()

    def begin_picked(step, _):
        copy_of(1, picked, picked_out, step).start()
        return 0

    lax.fori_loop(1, devices, begin_picked, 0)
    keep = pltpu.make_async_copy(picked.at[me], picked_out.at[me], own.at[3])
    keep.start()
    keep.wait()
    for step in range(1, lines):
        along_line(0, aperture_ref, apertures, step).wait_send()
        along_line(1, traces_here, traces, step).wait_send()

    def finish(step, _):
        copy_of(0, spectra_ref, spectra_out, step).wait_send()
        copy_of(1, picked, picked_out, step).wait_send()
        arrival_of(1, picked_out, step).wait_recv()
        return 0

    def arrived(step, _):
        arrival_of(0, spectra_out, step).wait_recv()
        return 0

    lax.fori_loop(2, devices, arrived, 0)
    lax.fori_loop(1, devices, finish, 0)


def collect_kernel(lines, columns, running_ref, out_ref, send, recv, own):
    line = lax.axis_index("xline")
    me = lax.axis_index("shot")
    core_line = line + 1 - 2 * lax.rem(line, 2)
    far_line = lax.rem(line + lines // 2, lines)
    diagonal_line = lax.rem(core_line + lines // 2, lines)
    mesh_id = pl.DeviceIdType.MESH
    barrier = pltpu.get_barrier_semaphore()

    def greet(step, _):
        pl.semaphore_signal(
            barrier, inc=1, device_id={"shot": lax.rem(me + step, columns)}, device_id_type=mesh_id
        )
        return 0

    lax.fori_loop(1, columns, greet, 0)
    for peer in (core_line, far_line):
        pl.semaphore_signal(barrier, inc=1, device_id={"xline": peer}, device_id_type=mesh_id)
    pl.semaphore_wait(barrier, columns + 1)

    def across(step):
        peer = lax.rem(me + step, columns)
        return pltpu.make_async_remote_copy(
            src_ref=running_ref.at[peer],
            dst_ref=out_ref.at[line * columns + me],
            send_sem=send.at[0, step],
            recv_sem=recv.at[0, step],
            device_id={"shot": peer},
            device_id_type=mesh_id,
        )

    def onward(stage, source_line, peer_line, step):
        slot = source_line * columns + lax.rem(me + columns - step, columns)
        return pltpu.make_async_remote_copy(
            src_ref=out_ref.at[slot],
            dst_ref=out_ref.at[slot],
            send_sem=send.at[stage, step],
            recv_sem=recv.at[stage, step],
            device_id={"xline": peer_line},
            device_id_type=mesh_id,
        )

    def begin(step, _):
        across(step).start()
        return 0

    lax.fori_loop(1, columns, begin, 0)
    mine = pltpu.make_async_copy(running_ref.at[me], out_ref.at[line * columns + me], own.at[0])
    mine.start()
    mine.wait()
    onward(2, line, far_line, 0).start()
    onward(1, line, core_line, 0).start()

    def relay(step, _):
        slot = line * columns + lax.rem(me + columns - step, columns)
        pltpu.make_async_remote_copy(
            src_ref=out_ref.at[slot],
            dst_ref=out_ref.at[slot],
            send_sem=send.at[0, step],
            recv_sem=recv.at[0, step],
            device_id={"shot": lax.rem(me + columns - step, columns)},
            device_id_type=mesh_id,
        ).wait_recv()
        onward(2, line, far_line, step).start()
        onward(1, line, core_line, step).start()
        return 0

    lax.fori_loop(1, columns, relay, 0)

    def turn(step, _):
        onward(2, far_line, far_line, step).wait_recv()
        onward(3, far_line, core_line, step).start()
        return 0

    lax.fori_loop(0, columns, turn, 0)

    def finish(step, _):
        onward(1, core_line, core_line, step).wait_recv()
        onward(3, diagonal_line, core_line, step).wait_recv()
        onward(1, line, core_line, step).wait_send()
        onward(2, line, far_line, step).wait_send()
        onward(3, far_line, core_line, step).wait_send()
        return 0

    lax.fori_loop(0, columns, finish, 0)

    def sent(step, _):
        across(step).wait_send()
        return 0

    lax.fori_loop(1, columns, sent, 0)


def on_device(records, targets, aperture):
    f32, bf16 = jnp.float32, jnp.bfloat16
    lines = lax.axis_size("xline")
    columns = lax.axis_size("shot")
    devices = lines * columns
    bins = NF // devices
    time_rows, shots, receivers = targets.shape
    held = records.shape[1]
    gathers = aperture.shape[2]
    table = fourier_table(bins, 0, NT).T
    chosen = shots * gathers

    spectra = jnp.einsum(
        "pt,kt->pk", table, records.reshape(held * receivers, NT), preferred_element_type=f32
    ).astype(bf16)

    spectra = spectra.reshape(devices, 2 * bins, held * receivers)
    in_vmem = pl.BlockSpec(memory_space=pltpu.VMEM)
    dma = pltpu.SemaphoreType.DMA
    spectra, picked = pl.pallas_call(
        functools.partial(spread_kernel, lines, columns, gathers),
        out_shape=[
            jax.ShapeDtypeStruct(spectra.shape, bf16),
            jax.ShapeDtypeStruct((devices, 2 * bins, chosen), bf16),
        ],
        in_specs=[in_vmem] * 4,
        out_specs=[in_vmem] * 2,
        scratch_shapes=[
            pltpu.VMEM((lines, 1, chosen), jnp.int32),
            pltpu.VMEM((lines, time_rows, chosen), bf16),
            pltpu.VMEM((lines, time_rows, chosen), bf16),
            pltpu.VMEM((devices, 2 * bins, chosen), bf16),
            dma((2, devices)), dma((2, devices)), dma((4,)), dma((2, lines)), dma((2, lines)),
        ],
        compiler_params=pltpu.CompilerParams(collective_id=0, has_side_effects=True),
    )(spectra, targets.transpose(1, 0, 2), aperture.reshape(1, chosen), table)
    picked = picked.reshape(devices, 2, bins, chosen)
    picked = jnp.concatenate([picked[:, 0], picked[:, 1]], axis=-1)

    running = pl.pallas_call(
        functools.partial(mix_kernel, lines, columns, held, bins, shots),
        out_shape=jax.ShapeDtypeStruct((shots * 2 * columns * bins, receivers), bf16),
        in_specs=[pl.BlockSpec(memory_space=pltpu.VMEM)] * 2,
        out_specs=pl.BlockSpec(memory_space=pltpu.VMEM),
    )(spectra.reshape(2 * NF, held * receivers), picked.reshape(NF, -1))
    running = running.reshape(shots, 2, columns, bins, receivers).transpose(2, 0, 1, 3, 4)
    running = running.reshape(columns, shots, 2 * bins, receivers)
    running = pl.pallas_call(
        functools.partial(collect_kernel, lines, columns),
        out_shape=jax.ShapeDtypeStruct((devices, *running.shape[1:]), bf16),
        in_specs=[in_vmem],
        out_specs=in_vmem,
        scratch_shapes=[dma((4, columns)), dma((4, columns)), dma((1,))],
        compiler_params=pltpu.CompilerParams(collective_id=1, has_side_effects=True),
    )(running)
    running = running.transpose(0, 2, 1, 3).reshape(2 * NF, shots, receivers)

    rows = fourier_table(bins, lax.axis_index("xline") * time_rows, time_rows)
    out = jnp.einsum("tp,psr->tsr", rows * 2, running, preferred_element_type=f32)
    return out.astype(bf16)


def solution(mesh):
    in_specs = (P("xline", "shot", None, None), P("xline", "shot", None), P("shot", "xline", None))
    out_specs = P("xline", "shot", None)
    return jax.shard_map(
        on_device, mesh=mesh, in_specs=in_specs, out_specs=out_specs, check_vma=False
    )
```

```python
import functools
import math

import jax
import jax.numpy as jnp
from jax import lax
from jax.experimental import pallas as pl
from jax.experimental.pallas import tpu as pltpu
from jax.sharding import PartitionSpec as P

NT = 2048
NF = 256
LOW = 32


def fourier_table(bins, start, count):
    blocks = NF // bins
    freq = jnp.arange(1, NF + 1, dtype=jnp.int32).reshape(blocks, 1, bins)
    freq = jnp.broadcast_to(freq, (blocks, 2, bins)).reshape(1, 2 * NF)
    is_imag = jnp.arange(2, dtype=jnp.int32).reshape(1, 2, 1)
    is_imag = jnp.broadcast_to(is_imag, (blocks, 2, bins)).reshape(1, 2 * NF) == 1

    def trig(times):
        angles = (times[:, None] * freq % NT).astype(jnp.float32) * (2.0 * math.pi / NT)
        return jnp.cos(angles), jnp.sin(angles)

    cos_hi, sin_hi = trig(start + jnp.arange(count // LOW, dtype=jnp.int32) * LOW)
    cos_lo, sin_lo = trig(jnp.arange(LOW, dtype=jnp.int32))
    scale = 1.0 / math.sqrt(NT)
    first = jnp.where(is_imag, -sin_hi, cos_hi) * scale
    second = jnp.where(is_imag, -cos_hi, -sin_hi) * scale
    first, second, cos_lo, sin_lo = lax.optimization_barrier((first, second, cos_lo, sin_lo))
    table = first[:, None] * cos_lo[None] + second[:, None] * sin_lo[None]
    return table.reshape(count, 2 * NF).astype(jnp.bfloat16)


def table_kernel(first_ref, second_ref, cos_ref, sin_ref, out_ref):
    low = cos_ref.shape[1]
    for hi in range(first_ref.shape[1]):
        out_ref[:, hi * low : (hi + 1) * low] = (
            first_ref[:, hi : hi + 1] * cos_ref[...] + second_ref[:, hi : hi + 1] * sin_ref[...]
        ).astype(out_ref.dtype)


def transposed_table(bins):
    low, blocks = 128, NF // bins
    freq = jnp.arange(1, NF + 1, dtype=jnp.int32).reshape(blocks, 1, bins)
    freq = jnp.broadcast_to(freq, (blocks, 2, bins)).reshape(2 * NF, 1)
    is_imag = jnp.arange(2, dtype=jnp.int32).reshape(1, 2, 1)
    is_imag = jnp.broadcast_to(is_imag, (blocks, 2, bins)).reshape(2 * NF, 1) == 1

    def trig(times):
        angles = (freq * times[None, :] % NT).astype(jnp.float32) * (2.0 * math.pi / NT)
        return jnp.cos(angles), jnp.sin(angles)

    cos_hi, sin_hi = trig(jnp.arange(NT // low, dtype=jnp.int32) * low)
    cos_lo, sin_lo = trig(jnp.arange(low, dtype=jnp.int32))
    scale = 1.0 / math.sqrt(NT)
    first = jnp.where(is_imag, -sin_hi, cos_hi) * scale
    second = jnp.where(is_imag, -cos_hi, -sin_hi) * scale
    in_vmem = pl.BlockSpec(memory_space=pltpu.VMEM)
    return pl.pallas_call(
        table_kernel,
        out_shape=jax.ShapeDtypeStruct((2 * NF, NT), jnp.bfloat16),
        in_specs=[in_vmem] * 4,
        out_specs=in_vmem,
    )(first, second, cos_lo, sin_lo)


def mix_kernel(lines, columns, held, bins, shots, spectra_ref, picked_ref, out_ref):
    gathers = columns * held
    receivers = out_ref.shape[1]
    rows = columns * bins
    depth = columns * 2 * bins
    taken = 2 * shots * gathers
    wide = held * depth

    k = lax.broadcasted_iota(jnp.int32, (taken, wide), 0)
    j = lax.broadcasted_iota(jnp.int32, (taken, wide), 1)
    k_imag, k_shot, k_gather = k // (shots * gathers), k // gathers % shots, k % gathers
    j_held, j_column, j_imag = j // depth, j % depth // (2 * bins), j // bins % 2
    same = k_gather == j_column * held + j_held
    crossed = k_imag != j_imag
    expand = []
    for shot in range(shots):
        for part in range(2):
            hit = same & (k_shot == shot) & (crossed if part else ~crossed)
            value = jnp.where(hit, 1.0, 0.0)
            if part == 0:
                value = jnp.where(j_imag == 1, -value, value)
            expand.append(value.astype(jnp.bfloat16))
    bin_of_row = lax.broadcasted_iota(jnp.int32, (rows, wide), 0) % bins
    bin_of_column = lax.broadcasted_iota(jnp.int32, (rows, wide), 1) % bins
    same_bin = bin_of_row == bin_of_column

    total = jnp.zeros(out_ref.shape, jnp.float32)
    for line in range(lines):
        block = picked_ref[line * rows : (line + 1) * rows, :]
        mixing = [
            jnp.where(
                same_bin, jnp.dot(block, matrix, preferred_element_type=jnp.float32), 0.0
            ).astype(jnp.bfloat16)
            for matrix in expand
        ]
        held_rows = slice(line * depth, (line + 1) * depth)
        spectra = jnp.concatenate(
            [spectra_ref[held_rows, h * receivers : (h + 1) * receivers] for h in range(held)], axis=0
        )
        total += jnp.dot(
            jnp.concatenate(mixing, axis=0), spectra, preferred_element_type=jnp.float32
        )
    out_ref[...] = total.astype(out_ref.dtype)


def spread_kernel(
    lines, columns, gathers, spectra_ref, targets_ref, aperture_ref, table_ref,
    spectra_out, picked_out,
    apertures, traces_here, traces, picked, send, recv, own, line_send, line_recv,
):
    devices = lines * columns
    line = lax.axis_index("xline")
    shot_here = lax.axis_index("shot")
    shots, time_rows, receivers = targets_ref.shape
    chosen = shots * gathers
    me = lax.axis_index("xline") * columns + lax.axis_index("shot")
    mesh_id = pl.DeviceIdType.MESH
    barrier = pltpu.get_barrier_semaphore()

    def greet(step, _):
        peer = lax.rem(me + step, devices)
        pl.semaphore_signal(
            barrier, inc=1,
            device_id={"xline": peer // columns, "shot": lax.rem(peer, columns)},
            device_id_type=mesh_id,
        )
        return 0

    lax.fori_loop(1, devices, greet, 0)
    pl.semaphore_wait(barrier, devices - 1)

    def line_of(step):
        far, other = step // columns // 2, lax.rem(step // columns, 2)
        moved = lax.rem(line + far * (lines // 2), lines)
        return moved + other * (1 - 2 * lax.rem(moved, 2))

    def copy_of(which, source, target, step):
        peer = line_of(step) * columns + lax.rem(shot_here + step, columns)
        return pltpu.make_async_remote_copy(
            src_ref=source.at[peer],
            dst_ref=target.at[me],
            send_sem=send.at[which, step],
            recv_sem=recv.at[which, step],
            device_id={"xline": peer // columns, "shot": lax.rem(peer, columns)},
            device_id_type=mesh_id,
        )

    def arrival_of(which, target, step):
        origin = line_of(step) * columns + lax.rem(shot_here + devices - step, columns)
        return pltpu.make_async_remote_copy(
            src_ref=target.at[origin],
            dst_ref=target.at[origin],
            send_sem=send.at[which, step],
            recv_sem=recv.at[which, step],
            device_id={"xline": origin // columns, "shot": lax.rem(origin, columns)},
            device_id_type=mesh_id,
        )

    def along_line(which, source, target, step):
        peer = lax.rem(line + step, lines)
        return pltpu.make_async_remote_copy(
            src_ref=source.at[peer] if which else source,
            dst_ref=target.at[line],
            send_sem=line_send.at[which, step],
            recv_sem=line_recv.at[which, step],
            device_id={"xline": peer},
            device_id_type=mesh_id,
        )

    def from_line(which, target, step):
        origin = lax.rem(line + lines - step, lines)
        return pltpu.make_async_remote_copy(
            src_ref=target.at[origin],
            dst_ref=target.at[origin],
            send_sem=line_send.at[which, step],
            recv_sem=line_recv.at[which, step],
            device_id={"xline": origin},
            device_id_type=mesh_id,
        )

    def begin(step, _):
        copy_of(0, spectra_ref, spectra_out, step).start()
        return 0

    for step in range(1, lines):
        along_line(0, aperture_ref, apertures, step).start()
    lax.fori_loop(1, 2 * columns, begin, 0)
    mine = [
        pltpu.make_async_copy(aperture_ref, apertures.at[line], own.at[0]),
        pltpu.make_async_copy(spectra_ref.at[me], spectra_out.at[me], own.at[1]),
    ]
    for copy in mine:
        copy.start()
    for copy in mine:
        copy.wait()
    for step in range(1, lines):
        from_line(0, apertures, step).wait_recv()

    wanted = jnp.concatenate(
        [apertures[l, s : s + 1, :] for l in range(lines) for s in range(shots)], axis=1
    )
    lane = lax.broadcasted_iota(jnp.int32, (receivers, lines * chosen), 1)
    receiver = lax.broadcasted_iota(jnp.int32, (receivers, lines * chosen), 0)
    total = jnp.zeros((time_rows, lines * chosen), jnp.float32)
    for shot in range(shots):
        hit = (lane // gathers % shots == shot) & (receiver == wanted)
        onehot = jnp.where(hit, 1.0, 0.0).astype(jnp.bfloat16)
        total += jnp.dot(targets_ref[shot], onehot, preferred_element_type=jnp.float32)
    total = total.astype(jnp.bfloat16)
    for l in range(lines):
        traces_here[l] = total[:, l * chosen : (l + 1) * chosen]

    arrival_of(0, spectra_out, 1).wait_recv()
    for step in range(1, lines):
        along_line(1, traces_here, traces, step).start()
    lax.fori_loop(2 * columns, devices, begin, 0)
    keep = pltpu.make_async_copy(traces_here.at[line], traces.at[line], own.at[2])
    keep.start()
    keep.wait()
    for step in range(1, lines):
        from_line(1, traces, step).wait_recv()

    value = jnp.zeros((table_ref.shape[0], chosen), jnp.float32)
    for l in range(lines):
        value += jnp.dot(
            table_ref[:, l * time_rows : (l + 1) * time_rows], traces[l],
            preferred_element_type=jnp.float32,
        )
    picked[...] = value.astype(jnp.bfloat16).reshape(picked.shape)
    arrival_of(0, spectra_out, 2).wait_recv()

    def begin_picked(step, _):
        copy_of(1, picked, picked_out, step).start()
        return 0

    lax.fori_loop(1, devices, begin_picked, 0)
    keep = pltpu.make_async_copy(picked.at[me], picked_out.at[me], own.at[3])
    keep.start()
    keep.wait()
    for step in range(1, lines):
        along_line(0, aperture_ref, apertures, step).wait_send()
        along_line(1, traces_here, traces, step).wait_send()

    def finish(step, _):
        copy_of(0, spectra_ref, spectra_out, step).wait_send()
        copy_of(1, picked, picked_out, step).wait_send()
        arrival_of(1, picked_out, step).wait_recv()
        return 0

    def arrived(step, _):
        arrival_of(0, spectra_out, step).wait_recv()
        return 0

    lax.fori_loop(3, devices, arrived, 0)
    lax.fori_loop(1, devices, finish, 0)


def collect_kernel(lines, columns, running_ref, out_ref, send, recv, own):
    line = lax.axis_index("xline")
    me = lax.axis_index("shot")
    core_line = line + 1 - 2 * lax.rem(line, 2)
    far_line = lax.rem(line + lines // 2, lines)
    diagonal_line = lax.rem(core_line + lines // 2, lines)
    mesh_id = pl.DeviceIdType.MESH
    barrier = pltpu.get_barrier_semaphore()

    def greet(step, _):
        pl.semaphore_signal(
            barrier, inc=1, device_id={"shot": lax.rem(me + step, columns)}, device_id_type=mesh_id
        )
        return 0

    lax.fori_loop(1, columns, greet, 0)
    for peer in (core_line, far_line):
        pl.semaphore_signal(barrier, inc=1, device_id={"xline": peer}, device_id_type=mesh_id)
    pl.semaphore_wait(barrier, columns + 1)

    def across(step):
        peer = lax.rem(me + step, columns)
        return pltpu.make_async_remote_copy(
            src_ref=running_ref.at[peer],
            dst_ref=out_ref.at[line * columns + me],
            send_sem=send.at[0, step],
            recv_sem=recv.at[0, step],
            device_id={"shot": peer},
            device_id_type=mesh_id,
        )

    def onward(stage, source_line, peer_line, step):
        slot = source_line * columns + lax.rem(me + columns - step, columns)
        return pltpu.make_async_remote_copy(
            src_ref=out_ref.at[slot],
            dst_ref=out_ref.at[slot],
            send_sem=send.at[stage, step],
            recv_sem=recv.at[stage, step],
            device_id={"xline": peer_line},
            device_id_type=mesh_id,
        )

    def begin(step, _):
        across(step).start()
        return 0

    lax.fori_loop(1, columns, begin, 0)
    mine = pltpu.make_async_copy(running_ref.at[me], out_ref.at[line * columns + me], own.at[0])
    mine.start()
    mine.wait()
    onward(2, line, far_line, 0).start()
    onward(1, line, core_line, 0).start()

    def relay(step, _):
        slot = line * columns + lax.rem(me + columns - step, columns)
        pltpu.make_async_remote_copy(
            src_ref=out_ref.at[slot],
            dst_ref=out_ref.at[slot],
            send_sem=send.at[0, step],
            recv_sem=recv.at[0, step],
            device_id={"shot": lax.rem(me + columns - step, columns)},
            device_id_type=mesh_id,
        ).wait_recv()
        onward(2, line, far_line, step).start()
        onward(1, line, core_line, step).start()
        return 0

    lax.fori_loop(1, columns, relay, 0)

    def turn(step, _):
        onward(2, far_line, far_line, step).wait_recv()
        onward(3, far_line, core_line, step).start()
        return 0

    lax.fori_loop(0, columns, turn, 0)

    def finish(step, _):
        onward(1, core_line, core_line, step).wait_recv()
        onward(3, diagonal_line, core_line, step).wait_recv()
        onward(1, line, core_line, step).wait_send()
        onward(2, line, far_line, step).wait_send()
        onward(3, far_line, core_line, step).wait_send()
        return 0

    lax.fori_loop(0, columns, finish, 0)

    def sent(step, _):
        across(step).wait_send()
        return 0

    lax.fori_loop(1, columns, sent, 0)


def on_device(records, targets, aperture):
    f32, bf16 = jnp.float32, jnp.bfloat16
    lines = lax.axis_size("xline")
    columns = lax.axis_size("shot")
    devices = lines * columns
    bins = NF // devices
    time_rows, shots, receivers = targets.shape
    held = records.shape[1]
    gathers = aperture.shape[2]
    table = transposed_table(bins)
    chosen = shots * gathers

    spectra = jnp.einsum(
        "pt,kt->pk", table, records.reshape(held * receivers, NT), preferred_element_type=f32
    ).astype(bf16)

    spectra = spectra.reshape(devices, 2 * bins, held * receivers)
    in_vmem = pl.BlockSpec(memory_space=pltpu.VMEM)
    dma = pltpu.SemaphoreType.DMA
    spectra, picked = pl.pallas_call(
        functools.partial(spread_kernel, lines, columns, gathers),
        out_shape=[
            jax.ShapeDtypeStruct(spectra.shape, bf16),
            jax.ShapeDtypeStruct((devices, 2 * bins, chosen), bf16),
        ],
        in_specs=[in_vmem] * 4,
        out_specs=[in_vmem] * 2,
        scratch_shapes=[
            pltpu.VMEM((lines, shots, gathers), jnp.int32),
            pltpu.VMEM((lines, time_rows, chosen), bf16),
            pltpu.VMEM((lines, time_rows, chosen), bf16),
            pltpu.VMEM((devices, 2 * bins, chosen), bf16),
            dma((2, devices)), dma((2, devices)), dma((4,)), dma((2, lines)), dma((2, lines)),
        ],
        compiler_params=pltpu.CompilerParams(collective_id=0, has_side_effects=True),
    )(spectra, targets.transpose(1, 0, 2), aperture.reshape(shots, gathers), table)
    picked = picked.reshape(devices, 2, bins, chosen)
    picked = jnp.concatenate([picked[:, 0], picked[:, 1]], axis=-1)

    running = pl.pallas_call(
        functools.partial(mix_kernel, lines, columns, held, bins, shots),
        out_shape=jax.ShapeDtypeStruct((shots * 2 * columns * bins, receivers), bf16),
        in_specs=[pl.BlockSpec(memory_space=pltpu.VMEM)] * 2,
        out_specs=pl.BlockSpec(memory_space=pltpu.VMEM),
    )(spectra.reshape(2 * NF, held * receivers), picked.reshape(NF, -1))
    running = running.reshape(shots, 2, columns, bins, receivers).transpose(2, 0, 1, 3, 4)
    running = running.reshape(columns, shots, 2 * bins, receivers)
    running = pl.pallas_call(
        functools.partial(collect_kernel, lines, columns),
        out_shape=jax.ShapeDtypeStruct((devices, *running.shape[1:]), bf16),
        in_specs=[in_vmem],
        out_specs=in_vmem,
        scratch_shapes=[dma((4, columns)), dma((4, columns)), dma((1,))],
        compiler_params=pltpu.CompilerParams(collective_id=1, has_side_effects=True),
    )(running)
    running = running.transpose(0, 2, 1, 3).reshape(2 * NF, shots, receivers)

    rows = fourier_table(bins, lax.axis_index("xline") * time_rows, time_rows)
    out = jnp.einsum("tp,psr->tsr", rows * 2, running, preferred_element_type=f32)
    return out.astype(bf16)


def solution(mesh):
    in_specs = (P("xline", "shot", None, None), P("xline", "shot", None), P("shot", "xline", None))
    out_specs = P("xline", "shot", None)
    return jax.shard_map(
        on_device, mesh=mesh, in_specs=in_specs, out_specs=out_specs, check_vma=False
    )
```

```python
import functools
import math

import jax
import jax.numpy as jnp
from jax import lax
from jax.experimental import pallas as pl
from jax.experimental.pallas import tpu as pltpu
from jax.sharding import PartitionSpec as P

NT = 2048
NF = 256
LOW = 32


def fourier_table(bins, start, count):
    blocks = NF // bins
    freq = jnp.arange(1, NF + 1, dtype=jnp.int32).reshape(blocks, 1, bins)
    freq = jnp.broadcast_to(freq, (blocks, 2, bins)).reshape(1, 2 * NF)
    is_imag = jnp.arange(2, dtype=jnp.int32).reshape(1, 2, 1)
    is_imag = jnp.broadcast_to(is_imag, (blocks, 2, bins)).reshape(1, 2 * NF) == 1

    def trig(times):
        angles = (times[:, None] * freq % NT).astype(jnp.float32) * (2.0 * math.pi / NT)
        return jnp.cos(angles), jnp.sin(angles)

    cos_hi, sin_hi = trig(start + jnp.arange(count // LOW, dtype=jnp.int32) * LOW)
    cos_lo, sin_lo = trig(jnp.arange(LOW, dtype=jnp.int32))
    scale = 1.0 / math.sqrt(NT)
    first = jnp.where(is_imag, -sin_hi, cos_hi) * scale
    second = jnp.where(is_imag, -cos_hi, -sin_hi) * scale
    first, second, cos_lo, sin_lo = lax.optimization_barrier((first, second, cos_lo, sin_lo))
    table = first[:, None] * cos_lo[None] + second[:, None] * sin_lo[None]
    return table.reshape(count, 2 * NF).astype(jnp.bfloat16)


def mix_kernel(lines, columns, held, bins, shots, spectra_ref, picked_ref, out_ref):
    gathers = columns * held
    receivers = out_ref.shape[1]
    rows = columns * bins
    depth = columns * 2 * bins
    taken = 2 * shots * gathers
    wide = held * depth

    k = lax.broadcasted_iota(jnp.int32, (taken, wide), 0)
    j = lax.broadcasted_iota(jnp.int32, (taken, wide), 1)
    k_imag, k_shot, k_gather = k // (shots * gathers), k // gathers % shots, k % gathers
    j_held, j_column, j_imag = j // depth, j % depth // (2 * bins), j // bins % 2
    same = k_gather == j_column * held + j_held
    crossed = k_imag != j_imag
    expand = []
    for shot in range(shots):
        for part in range(2):
            hit = same & (k_shot == shot) & (crossed if part else ~crossed)
            value = jnp.where(hit, 1.0, 0.0)
            if part == 0:
                value = jnp.where(j_imag == 1, -value, value)
            expand.append(value.astype(jnp.bfloat16))
    bin_of_row = lax.broadcasted_iota(jnp.int32, (rows, wide), 0) % bins
    bin_of_column = lax.broadcasted_iota(jnp.int32, (rows, wide), 1) % bins
    same_bin = bin_of_row == bin_of_column

    total = jnp.zeros(out_ref.shape, jnp.float32)
    for line in range(lines):
        block = picked_ref[line * rows : (line + 1) * rows, :]
        mixing = [
            jnp.where(
                same_bin, jnp.dot(block, matrix, preferred_element_type=jnp.float32), 0.0
            ).astype(jnp.bfloat16)
            for matrix in expand
        ]
        held_rows = slice(line * depth, (line + 1) * depth)
        spectra = jnp.concatenate(
            [spectra_ref[held_rows, h * receivers : (h + 1) * receivers] for h in range(held)], axis=0
        )
        total += jnp.dot(
            jnp.concatenate(mixing, axis=0), spectra, preferred_element_type=jnp.float32
        )
    out_ref[...] = total.astype(out_ref.dtype)


def spread_kernel(
    lines, columns, gathers, spectra_ref, targets_ref, aperture_ref, table_ref,
    spectra_out, picked_out,
    apertures, traces_here, traces, picked, send, recv, own, line_send, line_recv,
):
    devices = lines * columns
    line = lax.axis_index("xline")
    shot_here = lax.axis_index("shot")
    shots, time_rows, receivers = targets_ref.shape
    width = traces.shape[2]
    me = lax.axis_index("xline") * columns + lax.axis_index("shot")
    mesh_id = pl.DeviceIdType.MESH
    barrier = pltpu.get_barrier_semaphore()

    def greet(step, _):
        peer = lax.rem(me + step, devices)
        pl.semaphore_signal(
            barrier, inc=1,
            device_id={"xline": peer // columns, "shot": lax.rem(peer, columns)},
            device_id_type=mesh_id,
        )
        return 0

    lax.fori_loop(1, devices, greet, 0)
    pl.semaphore_wait(barrier, devices - 1)

    def line_of(step):
        far, other = step // columns // 2, lax.rem(step // columns, 2)
        moved = lax.rem(line + far * (lines // 2), lines)
        return moved + other * (1 - 2 * lax.rem(moved, 2))

    def copy_of(which, source, target, step):
        peer = line_of(step) * columns + lax.rem(shot_here + step, columns)
        return pltpu.make_async_remote_copy(
            src_ref=source.at[peer],
            dst_ref=target.at[me],
            send_sem=send.at[which, step],
            recv_sem=recv.at[which, step],
            device_id={"xline": peer // columns, "shot": lax.rem(peer, columns)},
            device_id_type=mesh_id,
        )

    def arrival_of(which, target, step):
        origin = line_of(step) * columns + lax.rem(shot_here + devices - step, columns)
        return pltpu.make_async_remote_copy(
            src_ref=target.at[origin],
            dst_ref=target.at[origin],
            send_sem=send.at[which, step],
            recv_sem=recv.at[which, step],
            device_id={"xline": origin // columns, "shot": lax.rem(origin, columns)},
            device_id_type=mesh_id,
        )

    def along_line(which, source, target, step):
        peer = lax.rem(line + step, lines)
        return pltpu.make_async_remote_copy(
            src_ref=source.at[peer] if which else source,
            dst_ref=target.at[line],
            send_sem=line_send.at[which, step],
            recv_sem=line_recv.at[which, step],
            device_id={"xline": peer},
            device_id_type=mesh_id,
        )

    def from_line(which, target, step):
        origin = lax.rem(line + lines - step, lines)
        return pltpu.make_async_remote_copy(
            src_ref=target.at[origin],
            dst_ref=target.at[origin],
            send_sem=line_send.at[which, step],
            recv_sem=line_recv.at[which, step],
            device_id={"xline": origin},
            device_id_type=mesh_id,
        )

    def begin(step, _):
        copy_of(0, spectra_ref, spectra_out, step).start()
        return 0

    for step in range(1, lines):
        along_line(0, aperture_ref, apertures, step).start()
    lax.fori_loop(1, 2 * columns, begin, 0)
    mine = [
        pltpu.make_async_copy(aperture_ref, apertures.at[line], own.at[0]),
        pltpu.make_async_copy(spectra_ref.at[me], spectra_out.at[me], own.at[1]),
    ]
    for copy in mine:
        copy.start()
    for copy in mine:
        copy.wait()
    for step in range(1, lines):
        from_line(0, apertures, step).wait_recv()

    wanted = []
    for l in range(lines):
        wanted += [apertures[l, s : s + 1, :] for s in range(shots)]
        if width > shots * gathers:
            wanted.append(jnp.zeros((1, width - shots * gathers), jnp.int32))
    wanted = jnp.concatenate(wanted, axis=1)
    lane = lax.broadcasted_iota(jnp.int32, (receivers, lines * width), 1)
    receiver = lax.broadcasted_iota(jnp.int32, (receivers, lines * width), 0)
    total = jnp.zeros((time_rows, lines * width), jnp.float32)
    for shot in range(shots):
        hit = (lane % width // gathers == shot) & (receiver == wanted)
        onehot = jnp.where(hit, 1.0, 0.0).astype(jnp.bfloat16)
        total += jnp.dot(targets_ref[shot], onehot, preferred_element_type=jnp.float32)
    total = total.astype(jnp.bfloat16)
    for l in range(lines):
        traces_here[l] = total[:, l * width : (l + 1) * width]

    arrival_of(0, spectra_out, 1).wait_recv()
    for step in range(1, lines):
        along_line(1, traces_here, traces, step).start()
    lax.fori_loop(2 * columns, devices, begin, 0)
    keep = pltpu.make_async_copy(traces_here.at[line], traces.at[line], own.at[2])
    keep.start()
    keep.wait()
    for step in range(1, lines):
        from_line(1, traces, step).wait_recv()

    value = jnp.zeros((table_ref.shape[0], width), jnp.float32)
    for l in range(lines):
        value += jnp.dot(
            table_ref[:, l * time_rows : (l + 1) * time_rows], traces[l],
            preferred_element_type=jnp.float32,
        )
    picked[...] = value.astype(jnp.bfloat16).reshape(picked.shape)
    arrival_of(0, spectra_out, 2).wait_recv()

    def begin_picked(step, _):
        copy_of(1, picked, picked_out, step).start()
        return 0

    lax.fori_loop(1, devices, begin_picked, 0)
    keep = pltpu.make_async_copy(picked.at[me], picked_out.at[me], own.at[3])
    keep.start()
    keep.wait()
    for step in range(1, lines):
        along_line(0, aperture_ref, apertures, step).wait_send()
        along_line(1, traces_here, traces, step).wait_send()

    def finish(step, _):
        copy_of(0, spectra_ref, spectra_out, step).wait_send()
        copy_of(1, picked, picked_out, step).wait_send()
        arrival_of(1, picked_out, step).wait_recv()
        return 0

    def arrived(step, _):
        arrival_of(0, spectra_out, step).wait_recv()
        return 0

    lax.fori_loop(3, devices, arrived, 0)
    lax.fori_loop(1, devices, finish, 0)


def collect_kernel(lines, columns, running_ref, out_ref, send, recv, own):
    line = lax.axis_index("xline")
    me = lax.axis_index("shot")
    core_line = line + 1 - 2 * lax.rem(line, 2)
    far_line = lax.rem(line + lines // 2, lines)
    diagonal_line = lax.rem(core_line + lines // 2, lines)
    mesh_id = pl.DeviceIdType.MESH
    barrier = pltpu.get_barrier_semaphore()

    def greet(step, _):
        pl.semaphore_signal(
            barrier, inc=1, device_id={"shot": lax.rem(me + step, columns)}, device_id_type=mesh_id
        )
        return 0

    lax.fori_loop(1, columns, greet, 0)
    for peer in (core_line, far_line):
        pl.semaphore_signal(barrier, inc=1, device_id={"xline": peer}, device_id_type=mesh_id)
    pl.semaphore_wait(barrier, columns + 1)

    def across(step):
        peer = lax.rem(me + step, columns)
        return pltpu.make_async_remote_copy(
            src_ref=running_ref.at[peer],
            dst_ref=out_ref.at[line * columns + me],
            send_sem=send.at[0, step],
            recv_sem=recv.at[0, step],
            device_id={"shot": peer},
            device_id_type=mesh_id,
        )

    def onward(stage, source_line, peer_line, step):
        slot = source_line * columns + lax.rem(me + columns - step, columns)
        return pltpu.make_async_remote_copy(
            src_ref=out_ref.at[slot],
            dst_ref=out_ref.at[slot],
            send_sem=send.at[stage, step],
            recv_sem=recv.at[stage, step],
            device_id={"xline": peer_line},
            device_id_type=mesh_id,
        )

    def begin(step, _):
        across(step).start()
        return 0

    lax.fori_loop(1, columns, begin, 0)
    mine = pltpu.make_async_copy(running_ref.at[me], out_ref.at[line * columns + me], own.at[0])
    mine.start()
    mine.wait()
    onward(2, line, far_line, 0).start()
    onward(1, line, core_line, 0).start()

    def relay(step, _):
        slot = line * columns + lax.rem(me + columns - step, columns)
        pltpu.make_async_remote_copy(
            src_ref=out_ref.at[slot],
            dst_ref=out_ref.at[slot],
            send_sem=send.at[0, step],
            recv_sem=recv.at[0, step],
            device_id={"shot": lax.rem(me + columns - step, columns)},
            device_id_type=mesh_id,
        ).wait_recv()
        onward(2, line, far_line, step).start()
        onward(1, line, core_line, step).start()
        return 0

    lax.fori_loop(1, columns, relay, 0)

    def turn(step, _):
        onward(2, far_line, far_line, step).wait_recv()
        onward(3, far_line, core_line, step).start()
        return 0

    lax.fori_loop(0, columns, turn, 0)

    def finish(step, _):
        onward(1, core_line, core_line, step).wait_recv()
        onward(3, diagonal_line, core_line, step).wait_recv()
        onward(1, line, core_line, step).wait_send()
        onward(2, line, far_line, step).wait_send()
        onward(3, far_line, core_line, step).wait_send()
        return 0

    lax.fori_loop(0, columns, finish, 0)

    def sent(step, _):
        across(step).wait_send()
        return 0

    lax.fori_loop(1, columns, sent, 0)


def on_device(records, targets, aperture):
    f32, bf16 = jnp.float32, jnp.bfloat16
    lines = lax.axis_size("xline")
    columns = lax.axis_size("shot")
    devices = lines * columns
    bins = NF // devices
    time_rows, shots, receivers = targets.shape
    held = records.shape[1]
    gathers = aperture.shape[2]
    table = fourier_table(bins, 0, NT).T
    chosen = shots * gathers
    padded = -(-chosen // 128) * 128

    spectra = jnp.einsum(
        "pt,kt->pk", table, records.reshape(held * receivers, NT), preferred_element_type=f32
    ).astype(bf16)

    spectra = spectra.reshape(devices, 2 * bins, held * receivers)
    in_vmem = pl.BlockSpec(memory_space=pltpu.VMEM)
    dma = pltpu.SemaphoreType.DMA
    spectra, picked = pl.pallas_call(
        functools.partial(spread_kernel, lines, columns, gathers),
        out_shape=[
            jax.ShapeDtypeStruct(spectra.shape, bf16),
            jax.ShapeDtypeStruct((devices, 2 * bins, padded), bf16),
        ],
        in_specs=[in_vmem] * 4,
        out_specs=[in_vmem] * 2,
        scratch_shapes=[
            pltpu.VMEM((lines, shots, gathers), jnp.int32),
            pltpu.VMEM((lines, time_rows, padded), bf16),
            pltpu.VMEM((lines, time_rows, padded), bf16),
            pltpu.VMEM((devices, 2 * bins, padded), bf16),
            dma((2, devices)), dma((2, devices)), dma((4,)), dma((2, lines)), dma((2, lines)),
        ],
        compiler_params=pltpu.CompilerParams(collective_id=0, has_side_effects=True),
    )(spectra, targets.transpose(1, 0, 2), aperture.reshape(shots, gathers), table)
    picked = picked.reshape(devices, 2, bins, padded)[..., :chosen]
    picked = jnp.concatenate([picked[:, 0], picked[:, 1]], axis=-1)

    running = pl.pallas_call(
        functools.partial(mix_kernel, lines, columns, held, bins, shots),
        out_shape=jax.ShapeDtypeStruct((shots * 2 * columns * bins, receivers), bf16),
        in_specs=[pl.BlockSpec(memory_space=pltpu.VMEM)] * 2,
        out_specs=pl.BlockSpec(memory_space=pltpu.VMEM),
    )(spectra.reshape(2 * NF, held * receivers), picked.reshape(NF, -1))
    running = running.reshape(shots, 2, columns, bins, receivers).transpose(2, 0, 1, 3, 4)
    running = running.reshape(columns, shots, 2 * bins, receivers)
    running = pl.pallas_call(
        functools.partial(collect_kernel, lines, columns),
        out_shape=jax.ShapeDtypeStruct((devices, *running.shape[1:]), bf16),
        in_specs=[in_vmem],
        out_specs=in_vmem,
        scratch_shapes=[dma((4, columns)), dma((4, columns)), dma((1,))],
        compiler_params=pltpu.CompilerParams(collective_id=1, has_side_effects=True),
    )(running)
    running = running.transpose(0, 2, 1, 3).reshape(2 * NF, shots, receivers)

    rows = fourier_table(bins, lax.axis_index("xline") * time_rows, time_rows)
    out = jnp.einsum("tp,psr->tsr", rows * 2, running, preferred_element_type=f32)
    return out.astype(bf16)


def solution(mesh):
    in_specs = (P("xline", "shot", None, None), P("xline", "shot", None), P("shot", "xline", None))
    out_specs = P("xline", "shot", None)
    return jax.shard_map(
        on_device, mesh=mesh, in_specs=in_specs, out_specs=out_specs, check_vma=False
    )
```

```python
import functools
import math

import jax
import jax.numpy as jnp
from jax import lax
from jax.experimental import pallas as pl
from jax.experimental.pallas import tpu as pltpu
from jax.sharding import PartitionSpec as P

NT = 2048
NF = 256
LOW = 32


def fourier_table(bins, start, count):
    blocks = NF // bins
    freq = jnp.arange(1, NF + 1, dtype=jnp.int32).reshape(blocks, 1, bins)
    freq = jnp.broadcast_to(freq, (blocks, 2, bins)).reshape(1, 2 * NF)
    is_imag = jnp.arange(2, dtype=jnp.int32).reshape(1, 2, 1)
    is_imag = jnp.broadcast_to(is_imag, (blocks, 2, bins)).reshape(1, 2 * NF) == 1

    def trig(times):
        angles = (times[:, None] * freq % NT).astype(jnp.float32) * (2.0 * math.pi / NT)
        return jnp.cos(angles), jnp.sin(angles)

    cos_hi, sin_hi = trig(start + jnp.arange(count // LOW, dtype=jnp.int32) * LOW)
    cos_lo, sin_lo = trig(jnp.arange(LOW, dtype=jnp.int32))
    scale = 1.0 / math.sqrt(NT)
    first = jnp.where(is_imag, -sin_hi, cos_hi) * scale
    second = jnp.where(is_imag, -cos_hi, -sin_hi) * scale
    first, second, cos_lo, sin_lo = lax.optimization_barrier((first, second, cos_lo, sin_lo))
    table = first[:, None] * cos_lo[None] + second[:, None] * sin_lo[None]
    return table.reshape(count, 2 * NF).astype(jnp.bfloat16)


def mix_kernel(lines, columns, held, bins, shots, spectra_ref, picked_ref, out_ref):
    gathers = columns * held
    receivers = out_ref.shape[1]
    rows = columns * bins
    depth = columns * 2 * bins
    taken = 2 * shots * gathers
    wide = held * depth

    k = lax.broadcasted_iota(jnp.int32, (taken, wide), 0)
    j = lax.broadcasted_iota(jnp.int32, (taken, wide), 1)
    k_imag, k_shot, k_gather = k // (shots * gathers), k // gathers % shots, k % gathers
    j_held, j_column, j_imag = j // depth, j % depth // (2 * bins), j // bins % 2
    same = k_gather == j_column * held + j_held
    crossed = k_imag != j_imag
    expand = []
    for shot in range(shots):
        for part in range(2):
            hit = same & (k_shot == shot) & (crossed if part else ~crossed)
            value = jnp.where(hit, 1.0, 0.0)
            if part == 0:
                value = jnp.where(j_imag == 1, -value, value)
            expand.append(value.astype(jnp.bfloat16))
    bin_of_row = lax.broadcasted_iota(jnp.int32, (rows, wide), 0) % bins
    bin_of_column = lax.broadcasted_iota(jnp.int32, (rows, wide), 1) % bins
    same_bin = bin_of_row == bin_of_column

    total = jnp.zeros(out_ref.shape, jnp.float32)
    for line in range(lines):
        block = picked_ref[line * rows : (line + 1) * rows, :]
        mixing = [
            jnp.where(
                same_bin, jnp.dot(block, matrix, preferred_element_type=jnp.float32), 0.0
            ).astype(jnp.bfloat16)
            for matrix in expand
        ]
        held_rows = slice(line * depth, (line + 1) * depth)
        spectra = jnp.concatenate(
            [spectra_ref[held_rows, h * receivers : (h + 1) * receivers] for h in range(held)], axis=0
        )
        total += jnp.dot(
            jnp.concatenate(mixing, axis=0), spectra, preferred_element_type=jnp.float32
        )
    out_ref[...] = total.astype(out_ref.dtype)


def spread_kernel(
    lines, columns, gathers, spectra_ref, targets_ref, aperture_ref, table_ref,
    spectra_out, picked_out,
    apertures, traces_here, traces, picked, send, recv, own, line_send, line_recv,
):
    devices = lines * columns
    line = lax.axis_index("xline")
    shot_here = lax.axis_index("shot")
    shots, time_rows, receivers = targets_ref.shape
    width = traces.shape[2]
    me = lax.axis_index("xline") * columns + lax.axis_index("shot")
    mesh_id = pl.DeviceIdType.MESH
    barrier = pltpu.get_barrier_semaphore()

    def greet(step, _):
        peer = lax.rem(me + step, devices)
        pl.semaphore_signal(
            barrier, inc=1,
            device_id={"xline": peer // columns, "shot": lax.rem(peer, columns)},
            device_id_type=mesh_id,
        )
        return 0

    lax.fori_loop(1, devices, greet, 0)
    pl.semaphore_wait(barrier, devices - 1)

    def line_of(step):
        far, other = step // columns // 2, lax.rem(step // columns, 2)
        moved = lax.rem(line + far * (lines // 2), lines)
        return moved + other * (1 - 2 * lax.rem(moved, 2))

    def copy_of(which, source, target, step):
        peer = line_of(step) * columns + lax.rem(shot_here + step, columns)
        return pltpu.make_async_remote_copy(
            src_ref=source.at[peer],
            dst_ref=target.at[me],
            send_sem=send.at[which, step],
            recv_sem=recv.at[which, step],
            device_id={"xline": peer // columns, "shot": lax.rem(peer, columns)},
            device_id_type=mesh_id,
        )

    def arrival_of(which, target, step):
        origin = line_of(step) * columns + lax.rem(shot_here + devices - step, columns)
        return pltpu.make_async_remote_copy(
            src_ref=target.at[origin],
            dst_ref=target.at[origin],
            send_sem=send.at[which, step],
            recv_sem=recv.at[which, step],
            device_id={"xline": origin // columns, "shot": lax.rem(origin, columns)},
            device_id_type=mesh_id,
        )

    def along_line(which, source, target, step):
        peer = lax.rem(line + step, lines)
        return pltpu.make_async_remote_copy(
            src_ref=source.at[peer] if which else source,
            dst_ref=target.at[line],
            send_sem=line_send.at[which, step],
            recv_sem=line_recv.at[which, step],
            device_id={"xline": peer},
            device_id_type=mesh_id,
        )

    def from_line(which, target, step):
        origin = lax.rem(line + lines - step, lines)
        return pltpu.make_async_remote_copy(
            src_ref=target.at[origin],
            dst_ref=target.at[origin],
            send_sem=line_send.at[which, step],
            recv_sem=line_recv.at[which, step],
            device_id={"xline": origin},
            device_id_type=mesh_id,
        )

    def begin(step, _):
        copy_of(0, spectra_ref, spectra_out, step).start()
        return 0

    for step in range(1, lines):
        along_line(0, aperture_ref, apertures, step).start()
    lax.fori_loop(1, 2 * columns, begin, 0)
    mine = [
        pltpu.make_async_copy(aperture_ref, apertures.at[line], own.at[0]),
        pltpu.make_async_copy(spectra_ref.at[me], spectra_out.at[me], own.at[1]),
    ]
    for copy in mine:
        copy.start()
    for copy in mine:
        copy.wait()
    for step in range(1, lines):
        from_line(0, apertures, step).wait_recv()

    wanted = []
    for l in range(lines):
        wanted += [apertures[l, s : s + 1, :] for s in range(shots)]
        if width > shots * gathers:
            wanted.append(jnp.zeros((1, width - shots * gathers), jnp.int32))
    wanted = jnp.concatenate(wanted, axis=1)
    lane = lax.broadcasted_iota(jnp.int32, (receivers, lines * width), 1)
    receiver = lax.broadcasted_iota(jnp.int32, (receivers, lines * width), 0)
    total = jnp.zeros((time_rows, lines * width), jnp.float32)
    for shot in range(shots):
        hit = (lane % width // gathers == shot) & (receiver == wanted)
        onehot = jnp.where(hit, 1.0, 0.0).astype(jnp.bfloat16)
        total += jnp.dot(targets_ref[shot], onehot, preferred_element_type=jnp.float32)
    total = total.astype(jnp.bfloat16)
    for l in range(lines):
        traces_here[l] = total[:, l * width : (l + 1) * width]

    arrival_of(0, spectra_out, 1).wait_recv()
    for step in range(1, lines):
        along_line(1, traces_here, traces, step).start()
    lax.fori_loop(2 * columns, devices, begin, 0)
    keep = pltpu.make_async_copy(traces_here.at[line], traces.at[line], own.at[2])
    keep.start()
    keep.wait()
    for step in range(1, lines):
        from_line(1, traces, step).wait_recv()

    value = jnp.zeros((table_ref.shape[1], width), jnp.float32)
    for l in range(lines):
        value += lax.dot_general(
            table_ref[l * time_rows : (l + 1) * time_rows, :], traces[l],
            (((0,), (0,)), ((), ())),
            preferred_element_type=jnp.float32,
        )
    picked[...] = value.astype(jnp.bfloat16).reshape(picked.shape)
    arrival_of(0, spectra_out, 2).wait_recv()

    def begin_picked(step, _):
        copy_of(1, picked, picked_out, step).start()
        return 0

    lax.fori_loop(1, devices, begin_picked, 0)
    keep = pltpu.make_async_copy(picked.at[me], picked_out.at[me], own.at[3])
    keep.start()
    keep.wait()
    for step in range(1, lines):
        along_line(0, aperture_ref, apertures, step).wait_send()
        along_line(1, traces_here, traces, step).wait_send()

    def finish(step, _):
        copy_of(0, spectra_ref, spectra_out, step).wait_send()
        copy_of(1, picked, picked_out, step).wait_send()
        arrival_of(1, picked_out, step).wait_recv()
        return 0

    def arrived(step, _):
        arrival_of(0, spectra_out, step).wait_recv()
        return 0

    lax.fori_loop(3, devices, arrived, 0)
    lax.fori_loop(1, devices, finish, 0)


def collect_kernel(lines, columns, running_ref, out_ref, send, recv, own):
    line = lax.axis_index("xline")
    me = lax.axis_index("shot")
    core_line = line + 1 - 2 * lax.rem(line, 2)
    far_line = lax.rem(line + lines // 2, lines)
    diagonal_line = lax.rem(core_line + lines // 2, lines)
    mesh_id = pl.DeviceIdType.MESH
    barrier = pltpu.get_barrier_semaphore()

    def greet(step, _):
        pl.semaphore_signal(
            barrier, inc=1, device_id={"shot": lax.rem(me + step, columns)}, device_id_type=mesh_id
        )
        return 0

    lax.fori_loop(1, columns, greet, 0)
    for peer in (core_line, far_line):
        pl.semaphore_signal(barrier, inc=1, device_id={"xline": peer}, device_id_type=mesh_id)
    pl.semaphore_wait(barrier, columns + 1)

    def across(step):
        peer = lax.rem(me + step, columns)
        return pltpu.make_async_remote_copy(
            src_ref=running_ref.at[peer],
            dst_ref=out_ref.at[line * columns + me],
            send_sem=send.at[0, step],
            recv_sem=recv.at[0, step],
            device_id={"shot": peer},
            device_id_type=mesh_id,
        )

    def onward(stage, source_line, peer_line, step):
        slot = source_line * columns + lax.rem(me + columns - step, columns)
        return pltpu.make_async_remote_copy(
            src_ref=out_ref.at[slot],
            dst_ref=out_ref.at[slot],
            send_sem=send.at[stage, step],
            recv_sem=recv.at[stage, step],
            device_id={"xline": peer_line},
            device_id_type=mesh_id,
        )

    def begin(step, _):
        across(step).start()
        return 0

    lax.fori_loop(1, columns, begin, 0)
    mine = pltpu.make_async_copy(running_ref.at[me], out_ref.at[line * columns + me], own.at[0])
    mine.start()
    mine.wait()
    onward(2, line, far_line, 0).start()
    onward(1, line, core_line, 0).start()

    def relay(step, _):
        slot = line * columns + lax.rem(me + columns - step, columns)
        pltpu.make_async_remote_copy(
            src_ref=out_ref.at[slot],
            dst_ref=out_ref.at[slot],
            send_sem=send.at[0, step],
            recv_sem=recv.at[0, step],
            device_id={"shot": lax.rem(me + columns - step, columns)},
            device_id_type=mesh_id,
        ).wait_recv()
        onward(2, line, far_line, step).start()
        onward(1, line, core_line, step).start()
        return 0

    lax.fori_loop(1, columns, relay, 0)

    def turn(step, _):
        onward(2, far_line, far_line, step).wait_recv()
        onward(3, far_line, core_line, step).start()
        return 0

    lax.fori_loop(0, columns, turn, 0)

    def finish(step, _):
        onward(1, core_line, core_line, step).wait_recv()
        onward(3, diagonal_line, core_line, step).wait_recv()
        onward(1, line, core_line, step).wait_send()
        onward(2, line, far_line, step).wait_send()
        onward(3, far_line, core_line, step).wait_send()
        return 0

    lax.fori_loop(0, columns, finish, 0)

    def sent(step, _):
        across(step).wait_send()
        return 0

    lax.fori_loop(1, columns, sent, 0)


def on_device(records, targets, aperture):
    f32, bf16 = jnp.float32, jnp.bfloat16
    lines = lax.axis_size("xline")
    columns = lax.axis_size("shot")
    devices = lines * columns
    bins = NF // devices
    time_rows, shots, receivers = targets.shape
    held = records.shape[1]
    gathers = aperture.shape[2]
    table = fourier_table(bins, 0, NT)
    chosen = shots * gathers
    padded = -(-chosen // 128) * 128

    spectra = jnp.einsum(
        "tp,kt->pk", table, records.reshape(held * receivers, NT), preferred_element_type=f32
    ).astype(bf16)

    spectra = spectra.reshape(devices, 2 * bins, held * receivers)
    in_vmem = pl.BlockSpec(memory_space=pltpu.VMEM)
    dma = pltpu.SemaphoreType.DMA
    spectra, picked = pl.pallas_call(
        functools.partial(spread_kernel, lines, columns, gathers),
        out_shape=[
            jax.ShapeDtypeStruct(spectra.shape, bf16),
            jax.ShapeDtypeStruct((devices, 2 * bins, padded), bf16),
        ],
        in_specs=[in_vmem] * 4,
        out_specs=[in_vmem] * 2,
        scratch_shapes=[
            pltpu.VMEM((lines, shots, gathers), jnp.int32),
            pltpu.VMEM((lines, time_rows, padded), bf16),
            pltpu.VMEM((lines, time_rows, padded), bf16),
            pltpu.VMEM((devices, 2 * bins, padded), bf16),
            dma((2, devices)), dma((2, devices)), dma((4,)), dma((2, lines)), dma((2, lines)),
        ],
        compiler_params=pltpu.CompilerParams(collective_id=0, has_side_effects=True),
    )(spectra, targets.transpose(1, 0, 2), aperture.reshape(shots, gathers), table)
    picked = picked.reshape(devices, 2, bins, padded)[..., :chosen]
    picked = jnp.concatenate([picked[:, 0], picked[:, 1]], axis=-1)

    running = pl.pallas_call(
        functools.partial(mix_kernel, lines, columns, held, bins, shots),
        out_shape=jax.ShapeDtypeStruct((shots * 2 * columns * bins, receivers), bf16),
        in_specs=[pl.BlockSpec(memory_space=pltpu.VMEM)] * 2,
        out_specs=pl.BlockSpec(memory_space=pltpu.VMEM),
    )(spectra.reshape(2 * NF, held * receivers), picked.reshape(NF, -1))
    running = running.reshape(shots, 2, columns, bins, receivers).transpose(2, 0, 1, 3, 4)
    running = running.reshape(columns, shots, 2 * bins, receivers)
    running = pl.pallas_call(
        functools.partial(collect_kernel, lines, columns),
        out_shape=jax.ShapeDtypeStruct((devices, *running.shape[1:]), bf16),
        in_specs=[in_vmem],
        out_specs=in_vmem,
        scratch_shapes=[dma((4, columns)), dma((4, columns)), dma((1,))],
        compiler_params=pltpu.CompilerParams(collective_id=1, has_side_effects=True),
    )(running)
    running = running.transpose(0, 2, 1, 3).reshape(2 * NF, shots, receivers)

    rows = fourier_table(bins, lax.axis_index("xline") * time_rows, time_rows)
    out = jnp.einsum("tp,psr->tsr", rows * 2, running, preferred_element_type=f32)
    return out.astype(bf16)


def solution(mesh):
    in_specs = (P("xline", "shot", None, None), P("xline", "shot", None), P("shot", "xline", None))
    out_specs = P("xline", "shot", None)
    return jax.shard_map(
        on_device, mesh=mesh, in_specs=in_specs, out_specs=out_specs, check_vma=False
    )
```
